256 devices in a mesh: text: 32 (over z_lo, y, core), video: 8 (over x, z_hi).
Axes of the slice: x: 4, y: 4, z: 8 (z_hi: 2, z_lo: 4; z = z_hi * 4 + z_lo), core: 2. Of those that a mesh axis runs over, the one named last changes fastest.
Arguments:
- queries: bfloat16 [4096, 4096], P('text'), may hold values from -53 to 53
- video_keys: bfloat16 [2048, 512], P('video'), may hold values from -6 to 6
- video_values: bfloat16 [2048, 512], P('video'), may hold values from -6 to 6
- grad_out: bfloat16 [4096, 4096], P('text'), may hold values from -6 to 6
- positions: int32 [4096], P('text'), may hold values from 1 to 2047, as said below
- span_bounds: int32 [32, 2], P('text'), may hold values from 0 to 2048, as said below
Outputs:
- attended: bfloat16 [4096, 4096], P('text', 'video')
- grad_query: bfloat16 [4096, 4096], P('text', 'video')
- grad_key: bfloat16 [2048, 512], P(('video', 'text'))
- grad_value: bfloat16 [2048, 512], P(('video', 'text'))
The draws below stay inside these ranges and needn't reach their ends.
Inputs may be any that keep to these rules, and one draw needn't show every extreme that they name: `span_bounds`: column 0 is a multiple of 128 from 0 to 384; column 1 is a multiple of 128 from 1664 to 2048. `positions`: each position is at least its block's span start plus 1.
All inputs are finite; a program needn't handle non-finite values.
Results may differ from the reference program's by a relative error of at most 0.017.
Values sent between devices are 32-bit elements; how exact they have to be, the bound alone decides.
No kernel may reach another device: no remote copies, remote signals or barrier semaphores. Data moves between devices by JAX's collectives and lax.ppermute only.
A program may use at most 128 MiB of HBM per device.

```python
import jax
import jax.numpy as jnp
from jax import lax

VID_DEV = 256
H = 32
G = 4
HD = 128
TBLK = 128
STEP = 128
TEXT = 4096
VTOK = 2048
NBLK = 32
N_VIDEO = 8


def span_table(key):
    base_key = jax.random.fold_in(key, 101)
    key_lower, key_upper, key_reach = jax.random.split(base_key, 3)
    quarter = VTOK // (4 * STEP)
    lower = STEP * jax.random.randint(key_lower, (NBLK,), 0, quarter)
    upper = VTOK - STEP * jax.random.randint(key_upper, (NBLK,), 0, quarter)
    lower = lower.at[0].set(0).at[1].set(VTOK // 4 - STEP)
    upper = upper.at[0].set(VTOK).at[1].set(3 * VTOK // 4 + STEP)
    lower_rows = jnp.repeat(lower, TBLK)
    reach = jax.random.randint(key_reach, (TEXT,), 0, VTOK - lower_rows - 1)
    places = lower_rows + 1 + reach
    places = places.at[0].set(1).at[1].set(VTOK - 1)
    return (lower.astype(jnp.int32), upper.astype(jnp.int32), places.astype(jnp.int32))


def key_table(key):
    base_key = jax.random.fold_in(key, 202)
    table = jax.random.truncated_normal(base_key, -6.0, 6.0, (VTOK, G * HD), jnp.float32)
    return table


def draw_video_keys(key, part):
    return key_table(key).astype(jnp.bfloat16)


def draw_positions(key, part):
    lower, upper, places = span_table(key)
    return places


def draw_span_bounds(key, part):
    lower, upper, places = span_table(key)
    return jnp.stack([lower, upper], axis=1).astype(jnp.int32)


def draw_queries(key, part):
    base_key = jax.random.fold_in(key, 303)
    key_normal = jax.random.fold_in(base_key, 0)
    table = jax.random.truncated_normal(key_normal, -6.0, 6.0, (TEXT, H * HD), jnp.float32)
    return table.astype(jnp.bfloat16)


def block_scale(own_key, extent, pieces, least, high):
    loudness, own = 1.0, jax.random.fold_in(own_key, 6)
    for position, parts in pieces:
        draws = jnp.exp(jax.random.uniform(jax.random.fold_in(own, position), (parts,), jnp.float32, least / len(pieces), high / len(pieces)))
        loudness = loudness * jnp.repeat(draws, extent[position] // parts).reshape([-1 if axis == position else 1 for axis in range(len(extent))])
    return loudness


def scatter_about(stream_key, dims, width, bound, pieces=(), kind=jnp.bfloat16):
    values = width * jax.random.normal(stream_key, dims, jnp.float32)
    if pieces:
        values = values * block_scale(stream_key, dims, pieces, -0.22, 0.18)
    return jnp.clip(values, -bound, bound).astype(kind)


def setup_inputs(seed: int = 0) -> dict:
    key_list = jax.random.split(jax.random.key(seed), 7)
    return {
        "queries": draw_queries(jax.random.fold_in(key_list[6], 71), 0),
        "video_keys": draw_video_keys(jax.random.fold_in(key_list[6], 71), 0),
        "video_values": scatter_about(key_list[2], (VTOK, G * HD), 1.0, 6.0, ((0, 8),)),
        "grad_out": scatter_about(key_list[3], (TEXT, H * HD), 1.0, 6.0, ((0, 32),)),
        "positions": draw_positions(jax.random.fold_in(key_list[6], 71), 0),
        "span_bounds": draw_span_bounds(jax.random.fold_in(key_list[6], 71), 0),
    }


masked_floor = -1.0e30


def hold_low(values):
    return lax.optimization_barrier(values.astype(jnp.bfloat16)).astype(jnp.float32)


def reference(queries, video_keys, video_values, grad_out, positions, span_bounds):
    score_scale = HD ** -0.5
    per_group = H // G
    columns = jnp.arange(VTOK, dtype=jnp.int32)
    keys_all = video_keys.astype(jnp.float32)
    values_all = video_values.astype(jnp.float32)
    block_count = TEXT // TBLK
    query_blocks = queries.reshape(block_count, TBLK, H * HD)
    grad_blocks = grad_out.reshape(block_count, TBLK, H * HD)
    position_blocks = positions.reshape(block_count, TBLK)

    def one_block(carry, items):
        key_total, value_total = carry
        query_rows, grad_rows, row_positions, bounds = items
        visible = (columns[None, :] >= bounds[0]) & (columns[None, :] < bounds[1]) & (columns[None, :] <= row_positions[:, None])
        vis_heads = visible[:, None, :]
        vis_blocks = vis_heads.reshape(TBLK, 1, N_VIDEO, VID_DEV)
        outs_att, outs_dq, outs_dk, outs_dv = [], [], [], []
        for group in range(G):
            head_start = group * per_group * HD
            head_stop = (group + 1) * per_group * HD
            query_grp = query_rows[:, head_start:head_stop].astype(jnp.float32).reshape(TBLK, per_group, HD)
            grad_grp = grad_rows[:, head_start:head_stop].astype(jnp.float32).reshape(TBLK, per_group, HD)
            key_grp = keys_all[:, group * HD:(group + 1) * HD]
            value_grp = values_all[:, group * HD:(group + 1) * HD]
            scores = jnp.einsum("rhd,cd->rhc", query_grp, key_grp) * score_scale
            masked = jnp.where(vis_heads, scores, masked_floor)
            masked_blocks = masked.reshape(TBLK, per_group, N_VIDEO, VID_DEV)
            block_peak = jnp.max(masked_blocks, axis=3)
            weights = jnp.where(vis_blocks, jnp.exp(masked_blocks - block_peak[..., None]), 0.0)
            block_total = jnp.sum(weights, axis=3)
            block_out = jnp.einsum("rhnc,ncd->rhnd", hold_low(weights), value_grp.reshape(N_VIDEO, VID_DEV, HD))
            row_peak = jnp.max(block_peak, axis=2)
            factor = jnp.exp(block_peak - row_peak[..., None])
            row_total = jnp.sum(block_total * factor, axis=2)
            numer = jnp.sum(block_out * factor[..., None], axis=2)
            attended = (numer / row_total[..., None]).astype(jnp.bfloat16)
            log_norm = row_peak + jnp.log(row_total)
            delta = jnp.sum(grad_grp * lax.optimization_barrier(attended).astype(jnp.float32), axis=2)
            prob = jnp.where(vis_heads, jnp.exp(masked - log_norm[..., None]), 0.0)
            dprob = jnp.einsum("rhd,cd->rhc", grad_grp, value_grp)
            dscore = hold_low(prob * (dprob - delta[..., None]))
            outs_att.append(attended.reshape(TBLK, per_group * HD))
            outs_dq.append(jnp.einsum("rhc,cd->rhd", dscore, key_grp).reshape(TBLK, per_group * HD) * score_scale)
            outs_dk.append(jnp.einsum("rhc,rhd->cd", dscore, query_grp) * score_scale)
            outs_dv.append(jnp.einsum("rhc,rhd->cd", hold_low(prob), grad_grp))
        key_total = key_total + jnp.concatenate(outs_dk, axis=1)
        value_total = value_total + jnp.concatenate(outs_dv, axis=1)
        att_rows = jnp.concatenate(outs_att, axis=1)
        dq_rows = jnp.concatenate(outs_dq, axis=1).astype(jnp.bfloat16)
        return (key_total, value_total), (att_rows, dq_rows)

    zeros = jnp.zeros((VTOK, G * HD), jnp.float32)
    (key_total, value_total), (att_blocks, dq_blocks) = lax.scan(one_block, (zeros, zeros), (query_blocks, grad_blocks, position_blocks, span_bounds))
    return (att_blocks.reshape(TEXT, H * HD), dq_blocks.reshape(TEXT, H * HD), key_total.astype(jnp.bfloat16), value_total.astype(jnp.bfloat16))
```

```python
import jax
import jax.numpy as jnp
from jax import lax
from jax.experimental import pallas as pl
from jax.experimental.pallas import tpu as pltpu
from jax.sharding import Mesh, PartitionSpec as P

H = 32
G = 4
HD = 128
ROWS = 128
HL = 4
VID = 256
TOK = 2048
HALF = TOK // 2
CH = 256
NCH = HALF // CH
R = HL * ROWS
SCALE = HD ** (-0.5)
LOG2E = 1.4426950408889634
FLOOR = -1e30

PLANE = ("zl", "y", "x", "zh")


def kernel(info, q_ref, g_ref, own_ref, oth_ref, pos_ref, att_ref, dq_ref, down_ref, doth_ref, s_ref, e_ref, k_ref, v_ref):
    f32, bf16 = jnp.float32, jnp.bfloat16
    core, low, top = info[0], info[1], info[2]
    last = jnp.minimum(pos_ref[...], top - 1)
    q = jnp.concatenate([q_ref[:, h * HD : (h + 1) * HD] for h in range(HL)], axis=0)
    halves = ((own_ref, down_ref), (oth_ref, doth_ref))

    peak = jnp.full((1, R), FLOOR, f32)
    for n in range(2 * NCH):
        half, j = divmod(n, NCH)
        src = halves[half][0]
        tiles = slice(j * (CH // 8), (j + 1) * (CH // 8))
        key = src[tiles, 0].reshape(CH, HD).astype(bf16)
        k_ref[n * CH : (n + 1) * CH, :] = key
        v_ref[n * CH : (n + 1) * CH, :] = src[tiles, 1].reshape(CH, HD).astype(bf16)
        cc = core if half == 0 else 1 - core
        i = lax.broadcasted_iota(jnp.int32, (CH, ROWS), 0) + j * CH
        col = (((i >> 3) & 7) << 8) + ((i >> 6) << 4) + (i & 7) + cc * 8
        vis = (col >= low) & (col <= last)
        s = lax.dot_general(key, q, (((1,), (1,)), ((), ())), preferred_element_type=f32)
        tops = []
        for h in range(HL):
            sh = jnp.where(vis, s[:, h * ROWS : (h + 1) * ROWS], FLOOR)
            s_ref[n * CH : (n + 1) * CH, h * ROWS : (h + 1) * ROWS] = sh
            tops.append(jnp.max(sh, axis=0, keepdims=True))
        peak = jnp.maximum(peak, jnp.concatenate(tops, axis=1))

    total = jnp.zeros((1, R), f32)
    out_t = jnp.zeros((HD, R), f32)
    for n in range(2 * NCH):
        rows = slice(n * CH, (n + 1) * CH)
        e = jnp.exp2((s_ref[rows, :] - peak) * (SCALE * LOG2E))
        total = total + jnp.sum(e, axis=0, keepdims=True)
        s_ref[rows, :] = e
        low_e = e.astype(bf16)
        e_ref[rows, :] = low_e
        out_t = out_t + jnp.dot(v_ref[rows, :].T, low_e, preferred_element_type=f32)

    inv = 1.0 / total
    att_t = (out_t * inv).astype(bf16)
    g_t = jnp.concatenate([g_ref[:, h * HD : (h + 1) * HD].T for h in range(HL)], axis=1).astype(f32)
    delta = jnp.sum(g_t * att_t.astype(f32), axis=0, keepdims=True) * inv
    for h in range(HL):
        att_ref[:, h * HD : (h + 1) * HD] = att_t[:, h * ROWS : (h + 1) * ROWS].T
    g_t = (g_t * inv).astype(bf16)

    dq_t = jnp.zeros((HD, R), f32)
    for n in range(2 * NCH):
        half, j = divmod(n, NCH)
        dst = halves[half][1]
        tiles = slice(j * (CH // 8), (j + 1) * (CH // 8))
        rows = slice(n * CH, (n + 1) * CH)
        dp = jnp.dot(v_ref[rows, :], g_t, preferred_element_type=f32)
        ds = (s_ref[rows, :] * (dp - delta)).astype(bf16)
        dk = jnp.dot(ds, q, preferred_element_type=f32) * SCALE
        dv = lax.dot_general(e_ref[rows, :], g_t, (((1,), (1,)), ((), ())), preferred_element_type=f32)
        dst[tiles, 0] = dk.reshape(CH // 8, 8, HD)
        dst[tiles, 1] = dv.reshape(CH // 8, 8, HD)
        dq_t = dq_t + jnp.dot(k_ref[rows, :].T, ds, preferred_element_type=f32)
    for h in range(HL):
        dq_ref[:, h * HD : (h + 1) * HD] = (dq_t[:, h * ROWS : (h + 1) * ROWS] * SCALE).T.astype(bf16)


def attend(info, queries, grad_out, own, oth, pos):
    shape = (HALF // 8, 2, 8, HD)
    whole = pl.BlockSpec(shape, lambda i, info: (0, 0, 0, 0))
    heads = pl.BlockSpec((ROWS, HL * HD), lambda i, info: (0, info[3]))
    flat = pl.BlockSpec((ROWS, HL * HD), lambda i, info: (0, 0))
    return pl.pallas_call(
        kernel,
        out_shape=(
            jax.ShapeDtypeStruct((ROWS, HL * HD), jnp.bfloat16),
            jax.ShapeDtypeStruct((ROWS, HL * HD), jnp.bfloat16),
            jax.ShapeDtypeStruct(shape, jnp.float32),
            jax.ShapeDtypeStruct(shape, jnp.float32),
        ),
        grid_spec=pltpu.PrefetchScalarGridSpec(
            num_scalar_prefetch=1,
            grid=(1,),
            in_specs=[heads, heads, whole, whole, pl.BlockSpec((1, ROWS), lambda i, info: (0, 0))],
            out_specs=(flat, flat, whole, whole),
            scratch_shapes=[
                pltpu.VMEM((TOK, R), jnp.float32),
                pltpu.VMEM((TOK, R), jnp.bfloat16),
                pltpu.VMEM((TOK, HD), jnp.bfloat16),
                pltpu.VMEM((TOK, HD), jnp.bfloat16),
            ],
        ),
        name="attend",
    )(info, queries, grad_out, own, oth, pos)


def swap(x):
    return lax.ppermute(x, "c", [(0, 1), (1, 0)])


def local(queries, video_keys, video_values, grad_out, positions, span_bounds):
    zl, y, c = lax.axis_index("zl"), lax.axis_index("y"), lax.axis_index("c")
    x, zh = lax.axis_index("x"), lax.axis_index("zh")
    t = (zl * 4 + y) * 2 + c
    share = jnp.stack(
        [lax.dynamic_slice_in_dim(a, t * 8, 8, 0) for a in (video_keys, video_values)]
    ).astype(jnp.float32)
    share = share.reshape(2, 8, G, HD).transpose(2, 0, 1, 3)
    send = jnp.broadcast_to(share[None, :, None], (16, G, 2, 2, 8, HD)).reshape(128, 2, 8, HD)
    own = lax.all_to_all(send, PLANE, 0, 0, tiled=True)
    oth = swap(own)
    info = jnp.stack([c, span_bounds[0, 0], span_bounds[0, 1], x * 2 + zh]).astype(jnp.int32)
    att, dq, down, doth = attend(info, queries, grad_out, own, oth, positions.reshape(1, ROWS))
    part = down + swap(doth)
    got = lax.all_to_all(part, PLANE, 0, 0, tiled=True)
    got = got.reshape(16, G, 2, 2, 8, HD)
    got = jnp.sum(got, axis=(0, 2))
    got = got.transpose(1, 2, 0, 3).reshape(2, 8, G * HD).astype(jnp.bfloat16)
    return att, dq, got[0], got[1]


def solution(mesh):
    fine = Mesh(mesh.devices.reshape(4, 4, 2, 4, 2), ("zl", "y", "c", "x", "zh"))
    text, video = ("zl", "y", "c"), ("x", "zh")
    return jax.shard_map(
        local,
        mesh=fine,
        in_specs=(P(text, None), P(video, None), P(video, None), P(text, None), P(text), P(text, None)),
        out_specs=(P(text, video), P(text, video), P(video + text, None), P(video + text, None)),
        check_vma=False,
    )
```

```python
import jax
import jax.numpy as jnp
from jax import lax
from jax.experimental import pallas as pl
from jax.experimental.pallas import tpu as pltpu
from jax.sharding import Mesh, PartitionSpec as P

G = 4
HD = 128
ROWS = 128
HL = 4
TOK = 2048
HALF = TOK // 2
CH = 256
NCH = HALF // CH
R = HL * ROWS
W = HL * HD
SCALE = HD ** (-0.5)
LOG2E = 1.4426950408889634
FLOOR = -1e30

AXES = ("za", "zb", "y", "c", "x", "zh")
NEAR = ("zb", "y", "x")
FAR = ("za", "zb", "zh")


def kernel(q_hbm, g_hbm, own_ref, oth_ref, pos_ref, span_ref, att_hbm, dq_hbm, down_ref, doth_ref,
           q_ref, g_ref, att_ref, dq_ref, s_ref, e_ref, k_ref, v_ref, sems):
    f32, bf16 = jnp.float32, jnp.bfloat16
    za, core, zh = lax.axis_index("za"), lax.axis_index("c"), lax.axis_index("zh")
    first = pl.multiple_of((lax.axis_index("x") * 2 + zh) * W, W)
    get_q = pltpu.make_async_copy(q_hbm.at[:, pl.ds(first, W)], q_ref, sems.at[0])
    get_g = pltpu.make_async_copy(g_hbm.at[:, pl.ds(first, W)], g_ref, sems.at[1])
    get_q.start()
    get_g.start()
    low, top = span_ref[0, 0], span_ref[0, 1]
    last = jnp.minimum(pos_ref[...], top - 1)
    halves = ((own_ref, down_ref), (oth_ref, doth_ref))
    get_q.wait()
    q = jnp.concatenate([q_ref[:, h * HD : (h + 1) * HD] for h in range(HL)], axis=0)

    peak = jnp.full((1, R), FLOOR, f32)
    for n in range(2 * NCH):
        half, j = divmod(n, NCH)
        src = halves[half][0]
        tiles = slice(j * (CH // 8), (j + 1) * (CH // 8))
        key = src[tiles, 0].reshape(CH, HD).astype(bf16)
        k_ref[n * CH : (n + 1) * CH, :] = key
        v_ref[n * CH : (n + 1) * CH, :] = src[tiles, 1].reshape(CH, HD).astype(bf16)
        cc = core if half == 0 else 1 - core
        i = lax.broadcasted_iota(jnp.int32, (CH, ROWS), 0) + j * CH
        block = (((i >> 5) & 3) << 1) + (((i >> 4) & 1) ^ zh)
        tile = ((((i >> 3) & 1) ^ za) << 4) + ((i >> 9) << 3) + (((i >> 7) & 3) << 1) + cc
        col = (block << 8) + (tile << 3) + (i & 7)
        vis = (col >= low) & (col <= last)
        s = lax.dot_general(key, q, (((1,), (1,)), ((), ())), preferred_element_type=f32)
        tops = []
        for h in range(HL):
            sh = jnp.where(vis, s[:, h * ROWS : (h + 1) * ROWS], FLOOR)
            s_ref[n * CH : (n + 1) * CH, h * ROWS : (h + 1) * ROWS] = sh
            tops.append(jnp.max(sh, axis=0, keepdims=True))
        peak = jnp.maximum(peak, jnp.concatenate(tops, axis=1))

    total = jnp.zeros((1, R), f32)
    out_t = jnp.zeros((HD, R), f32)
    for n in range(2 * NCH):
        rows = slice(n * CH, (n + 1) * CH)
        e = jnp.exp2((s_ref[rows, :] - peak) * (SCALE * LOG2E))
        total = total + jnp.sum(e, axis=0, keepdims=True)
        s_ref[rows, :] = e
        low_e = e.astype(bf16)
        e_ref[rows, :] = low_e
        out_t = out_t + jnp.dot(v_ref[rows, :].T, low_e, preferred_element_type=f32)

    inv = 1.0 / total
    att_t = (out_t * inv).astype(bf16)
    for h in range(HL):
        att_ref[:, h * HD : (h + 1) * HD] = att_t[:, h * ROWS : (h + 1) * ROWS].T
    put_att = pltpu.make_async_copy(att_ref, att_hbm, sems.at[2])
    put_att.start()
    get_g.wait()
    g_t = jnp.concatenate([g_ref[:, h * HD : (h + 1) * HD].T for h in range(HL)], axis=1).astype(f32)
    delta = jnp.sum(g_t * att_t.astype(f32), axis=0, keepdims=True) * inv
    g_t = (g_t * inv).astype(bf16)

    dq_t = jnp.zeros((HD, R), f32)
    for n in range(2 * NCH):
        half, j = divmod(n, NCH)
        dst = halves[half][1]
        tiles = slice(j * (CH // 8), (j + 1) * (CH // 8))
        rows = slice(n * CH, (n + 1) * CH)
        dp = jnp.dot(v_ref[rows, :], g_t, preferred_element_type=f32)
        ds = (s_ref[rows, :] * (dp - delta)).astype(bf16)
        dk = jnp.dot(ds, q, preferred_element_type=f32) * SCALE
        dv = lax.dot_general(e_ref[rows, :], g_t, (((1,), (1,)), ((), ())), preferred_element_type=f32)
        dst[tiles, 0] = dk.reshape(CH // 8, 8, HD)
        dst[tiles, 1] = dv.reshape(CH // 8, 8, HD)
        dq_t = dq_t + jnp.dot(k_ref[rows, :].T, ds, preferred_element_type=f32)
    for h in range(HL):
        dq_ref[:, h * HD : (h + 1) * HD] = (dq_t[:, h * ROWS : (h + 1) * ROWS] * SCALE).T.astype(bf16)
    put_dq = pltpu.make_async_copy(dq_ref, dq_hbm, sems.at[3])
    put_dq.start()
    put_att.wait()
    put_dq.wait()


def attend(queries, grad_out, own, oth, pos, span):
    shape = (HALF // 8, 2, 8, HD)
    far, near = pl.BlockSpec(memory_space=pl.ANY), pl.BlockSpec(memory_space=pltpu.VMEM)
    return pl.pallas_call(
        kernel,
        out_shape=(
            jax.ShapeDtypeStruct((ROWS, W), jnp.bfloat16),
            jax.ShapeDtypeStruct((ROWS, W), jnp.bfloat16),
            jax.ShapeDtypeStruct(shape, jnp.float32),
            jax.ShapeDtypeStruct(shape, jnp.float32),
        ),
        in_specs=[far, far, near, near, near, pl.BlockSpec(memory_space=pltpu.SMEM)],
        out_specs=(far, far, near, near),
        scratch_shapes=[
            pltpu.VMEM((ROWS, W), jnp.bfloat16),
            pltpu.VMEM((ROWS, W), jnp.bfloat16),
            pltpu.VMEM((ROWS, W), jnp.bfloat16),
            pltpu.VMEM((ROWS, W), jnp.bfloat16),
            pltpu.VMEM((TOK, R), jnp.float32),
            pltpu.VMEM((TOK, R), jnp.bfloat16),
            pltpu.VMEM((TOK, HD), jnp.bfloat16),
            pltpu.VMEM((TOK, HD), jnp.bfloat16),
            pltpu.SemaphoreType.DMA((4,)),
        ],
        compiler_params=pltpu.CompilerParams(vmem_limit_bytes=24 << 20),
        name="attend",
    )(queries, grad_out, own, oth, pos, span)


def swap(x):
    return lax.ppermute(x, "c", [(0, 1), (1, 0)])


def z_pairs(move):
    index = lambda z: ((z >> 1) & 1) * 4 + (z & 1) * 2 + (z >> 2)
    return [(index(z), index(move(z))) for z in range(8)]


def local(queries, video_keys, video_values, grad_out, positions, span_bounds):
    za, zb, y, c = (lax.axis_index(a) for a in ("za", "zb", "y", "c"))

    def tile(a, b):
        row = (((a * 2 + b) * 4 + y) * 2 + c) * 8
        pair = [lax.dynamic_slice_in_dim(t, row, 8, 0) for t in (video_keys, video_values)]
        return jnp.stack(pair).reshape(2, 8, G, HD).transpose(2, 0, 1, 3)

    other = jnp.stack([tile(1 - za, 1 - zb), tile(za, 1 - zb)], axis=1).astype(jnp.float32)
    other = lax.ppermute(other, FAR, z_pairs(lambda z: 7 - z))
    mine = jnp.stack([tile(za, zb), tile(1 - za, zb)], axis=1).astype(jnp.float32)
    send = jnp.stack([mine, other], axis=1)
    send = jnp.broadcast_to(send[None], (8, *send.shape)).reshape(128, 2, 8, HD)
    own = lax.all_to_all(send, NEAR, 0, 0, tiled=True)
    oth = swap(own)
    att, dq, down, doth = attend(queries, grad_out, own, oth, positions.reshape(1, ROWS), span_bounds)
    part = down + swap(doth)
    got = lax.all_to_all(part, NEAR, 0, 0, tiled=True)
    got = jnp.sum(got.reshape(8, G, 4, 2, 8, HD), axis=0)
    total = got[:, 0]
    for k, move in ((2, lambda z: z ^ 4), (1, lambda z: z ^ 2), (3, lambda z: z ^ 6)):
        total = total + lax.ppermute(got[:, k], FAR, z_pairs(move))
    total = total.transpose(1, 2, 0, 3).reshape(2, 8, G * HD).astype(jnp.bfloat16)
    return att, dq, total[0], total[1]


def solution(mesh):
    fine = Mesh(mesh.devices.reshape(2, 2, 4, 2, 4, 2), AXES)
    text, video = ("za", "zb", "y", "c"), ("x", "zh")
    return jax.shard_map(
        local,
        mesh=fine,
        in_specs=(P(text, None), P(video, None), P(video, None), P(text, None), P(text), P(text, None)),
        out_specs=(P(text, video), P(text, video), P(video + text, None), P(video + text, None)),
        check_vma=False,
    )
```

```python
import jax
import jax.numpy as jnp
from jax import lax
from jax.experimental import pallas as pl
from jax.experimental.pallas import tpu as pltpu
from jax.sharding import Mesh, PartitionSpec as P

G = 4
HD = 128
ROWS = 128
HL = 4
TOK = 2048
HALF = TOK // 2
CH = 256
TILES = CH // 8
R = HL * ROWS
W = HL * HD
SCALE = HD ** (-0.5)
LOG2E = 1.4426950408889634
FLOOR = -1e30
F32, BF16 = jnp.float32, jnp.bfloat16

AXES = ("za", "zb", "y", "c", "x", "zh")
NEAR = ("zb", "y", "x")
FAR = ("za", "zb", "zh")


def first_column():
    return pl.multiple_of((lax.axis_index("x") * 2 + lax.axis_index("zh")) * W, W)


def stacked(ref):
    return jnp.concatenate([ref[:, h * HD : (h + 1) * HD] for h in range(HL)], axis=0)


def forward(src, mate, q, pos_ref, span_ref, e_ref, k_ref, v_ref):
    za, zh, core = lax.axis_index("za"), lax.axis_index("zh"), lax.axis_index("c") ^ mate
    low, top = span_ref[0, 0], span_ref[0, 1]
    last = jnp.minimum(pos_ref[...], top - 1)
    peak = jnp.full((1, R), FLOOR, F32)
    for n in range(HALF // CH):
        tiles = slice(n * TILES, (n + 1) * TILES)
        rows = slice(n * CH, (n + 1) * CH)
        key = src[tiles, 0].reshape(CH, HD).astype(BF16)
        k_ref[rows, :] = key
        v_ref[rows, :] = src[tiles, 1].reshape(CH, HD).astype(BF16)
        i = lax.broadcasted_iota(jnp.int32, (CH, ROWS), 0) + n * CH
        block = (((i >> 5) & 3) << 1) + (((i >> 4) & 1) ^ zh)
        tile = ((((i >> 3) & 1) ^ za) << 4) + ((i >> 9) << 3) + (((i >> 7) & 3) << 1) + core
        col = (block << 8) + (tile << 3) + (i & 7)
        vis = (col >= low) & (col <= last)
        s = lax.dot_general(key, q, (((1,), (1,)), ((), ())), preferred_element_type=F32)
        tops = []
        for h in range(HL):
            sh = jnp.where(vis, s[:, h * ROWS : (h + 1) * ROWS], FLOOR)
            e_ref[rows, h * ROWS : (h + 1) * ROWS] = sh
            tops.append(jnp.max(sh, axis=0, keepdims=True))
        peak = jnp.maximum(peak, jnp.concatenate(tops, axis=1))
    total = jnp.zeros((1, R), F32)
    out_t = jnp.zeros((HD, R), F32)
    for n in range(HALF // CH):
        rows = slice(n * CH, (n + 1) * CH)
        e = jnp.exp2((e_ref[rows, :] - peak) * (SCALE * LOG2E))
        total = total + jnp.sum(e, axis=0, keepdims=True)
        e_ref[rows, :] = e
        out_t = out_t + jnp.dot(v_ref[rows, :].T, e.astype(BF16), preferred_element_type=F32)
    return peak, total, out_t


def backward(e_ref, k_ref, v_ref, q, g_t, delta, dst, dq_t):
    for n in range(HALF // CH):
        rows = slice(n * CH, (n + 1) * CH)
        tiles = slice(n * TILES, (n + 1) * TILES)
        e = e_ref[rows, :]
        dp = jnp.dot(v_ref[rows, :], g_t, preferred_element_type=F32)
        ds = (e * (dp - delta)).astype(BF16)
        dk = jnp.dot(ds, q, preferred_element_type=F32) * SCALE
        dv = lax.dot_general(e.astype(BF16), g_t, (((1,), (1,)), ((), ())), preferred_element_type=F32)
        dst[tiles, 0] = dk.reshape(TILES, 8, HD)
        dst[tiles, 1] = dv.reshape(TILES, 8, HD)
        dq_t = dq_t + jnp.dot(k_ref[rows, :].T, ds, preferred_element_type=F32)
    return dq_t


def first_kernel(q_hbm, own_ref, pos_ref, span_ref, e_ref, k_ref, v_ref, peak_ref, total_ref, out_ref, q_ref, sem):
    get_q = pltpu.make_async_copy(q_hbm.at[:, pl.ds(first_column(), W)], q_ref, sem)
    get_q.start()
    get_q.wait()
    peak, total, out_t = forward(own_ref, 0, stacked(q_ref), pos_ref, span_ref, e_ref, k_ref, v_ref)
    peak_ref[...], total_ref[...], out_ref[...] = peak, total, out_t


def second_kernel(q_hbm, g_hbm, oth_ref, pos_ref, span_ref, peak1_ref, total1_ref, out1_ref,
                  att_hbm, grad_ref, gt_ref, delta_ref, dq_ref, q_ref, g_ref, att_ref, e_ref, k_ref, v_ref, sems):
    get_q = pltpu.make_async_copy(q_hbm.at[:, pl.ds(first_column(), W)], q_ref, sems.at[0])
    get_g = pltpu.make_async_copy(g_hbm.at[:, pl.ds(first_column(), W)], g_ref, sems.at[1])
    get_q.start()
    get_g.start()
    get_q.wait()
    q = stacked(q_ref)
    peak2, total2, out2 = forward(oth_ref, 1, q, pos_ref, span_ref, e_ref, k_ref, v_ref)
    peak1 = peak1_ref[...]
    peak = jnp.maximum(peak1, peak2)
    part1 = jnp.exp2((peak1 - peak) * (SCALE * LOG2E))
    part2 = jnp.exp2((peak2 - peak) * (SCALE * LOG2E))
    inv = 1.0 / (total1_ref[...] * part1 + total2 * part2)
    part1, part2 = part1 * inv, part2 * inv
    att_t = (out1_ref[...] * part1 + out2 * part2).astype(BF16)
    for h in range(HL):
        att_ref[:, h * HD : (h + 1) * HD] = att_t[:, h * ROWS : (h + 1) * ROWS].T
    put_att = pltpu.make_async_copy(att_ref, att_hbm, sems.at[2])
    put_att.start()
    get_g.wait()
    g_t = jnp.concatenate([g_ref[:, h * HD : (h + 1) * HD].T for h in range(HL)], axis=1).astype(F32)
    delta = jnp.sum(g_t * att_t.astype(F32), axis=0, keepdims=True)
    gt_ref[...] = (g_t * part1).astype(BF16)
    delta_ref[...] = delta * part1
    dq_ref[...] = backward(e_ref, k_ref, v_ref, q, (g_t * part2).astype(BF16), delta * part2, grad_ref, jnp.zeros((HD, R), F32))
    put_att.wait()


def third_kernel(q_hbm, e_ref, k_ref, v_ref, gt_ref, delta_ref, dq0_ref, dq_hbm, grad_ref, q_ref, dq_ref, sems):
    get_q = pltpu.make_async_copy(q_hbm.at[:, pl.ds(first_column(), W)], q_ref, sems.at[0])
    get_q.start()
    get_q.wait()
    dq_t = backward(e_ref, k_ref, v_ref, stacked(q_ref), gt_ref[...], delta_ref[...], grad_ref, dq0_ref[...])
    for h in range(HL):
        dq_ref[:, h * HD : (h + 1) * HD] = (dq_t[:, h * ROWS : (h + 1) * ROWS] * SCALE).T.astype(BF16)
    put_dq = pltpu.make_async_copy(dq_ref, dq_hbm, sems.at[1])
    put_dq.start()
    put_dq.wait()


def call(body, name, outs, ins, spaces, out_spaces, scratch, flops):
    kinds = {"h": pl.ANY, "v": pltpu.VMEM, "s": pltpu.SMEM}
    return pl.pallas_call(
        body,
        out_shape=tuple(jax.ShapeDtypeStruct(shape, kind) for shape, kind in outs),
        in_specs=[pl.BlockSpec(memory_space=kinds[k]) for k in spaces],
        out_specs=tuple(pl.BlockSpec(memory_space=kinds[k]) for k in out_spaces),
        scratch_shapes=scratch,
        compiler_params=pltpu.CompilerParams(vmem_limit_bytes=16 << 20),
        cost_estimate=pl.CostEstimate(flops=flops, bytes_accessed=8 << 20, transcendentals=HALF * R),
        name=name,
    )(*ins)


def swap(x):
    return lax.ppermute(x, "c", [(0, 1), (1, 0)])


def z_pairs(move):
    index = lambda z: ((z >> 1) & 1) * 4 + (z & 1) * 2 + (z >> 2)
    return [(index(z), index(move(z))) for z in range(8)]


def local(queries, video_keys, video_values, grad_out, positions, span_bounds):
    za, zb, y, c = (lax.axis_index(a) for a in ("za", "zb", "y", "c"))
    pos = positions.reshape(1, ROWS)

    def tile(a, b):
        row = (((a * 2 + b) * 4 + y) * 2 + c) * 8
        pair = [lax.dynamic_slice_in_dim(t, row, 8, 0) for t in (video_keys, video_values)]
        return jnp.stack(pair).reshape(2, 8, G, HD).transpose(2, 0, 1, 3)

    other = jnp.stack([tile(1 - za, 1 - zb), tile(za, 1 - zb)], axis=1).astype(F32)
    other = lax.ppermute(other, FAR, z_pairs(lambda z: 7 - z))
    mine = jnp.stack([tile(za, zb), tile(1 - za, zb)], axis=1).astype(F32)
    send = jnp.stack([mine, other], axis=1)
    send = jnp.broadcast_to(send[None], (8, *send.shape)).reshape(128, 2, 8, HD)
    own = lax.all_to_all(send, NEAR, 0, 0, tiled=True)
    oth = swap(own)

    row = ((1, R), F32)
    wide = ((HD, R), F32)
    flat = ((ROWS, W), BF16)
    grad = ((128, 2, 8, HD), F32)
    half = [((HALF, R), F32), ((HALF, HD), BF16), ((HALF, HD), BF16)]
    block = pltpu.VMEM((ROWS, W), BF16)
    e, k, v, peak, total, out = call(
        first_kernel, "first", half + [row, row, wide], (queries, own, pos, span_bounds), "hvvs", "vvvvvv",
        [block, pltpu.SemaphoreType.DMA], 4 * HALF * R * HD)
    att, doth, gt, delta, dq = call(
        second_kernel, "second", [flat, grad, ((HD, R), BF16), row, wide],
        (queries, grad_out, oth, pos, span_bounds, peak, total, out), "hhvvsvvv", "hvvvv",
        [block, block, block, *(pltpu.VMEM(*h) for h in half), pltpu.SemaphoreType.DMA((3,))], 12 * HALF * R * HD)
    doth = swap(doth)
    dq, down = call(
        third_kernel, "third", [flat, grad], (queries, e, k, v, gt, delta, dq), "hvvvvvv", "hv",
        [block, block, pltpu.SemaphoreType.DMA((2,))], 8 * HALF * R * HD)
    part = down + doth
    got = lax.all_to_all(part, NEAR, 0, 0, tiled=True)
    got = jnp.sum(got.reshape(8, G, 4, 2, 8, HD), axis=0)
    total = got[:, 0]
    for i, move in ((2, lambda z: z ^ 4), (1, lambda z: z ^ 2), (3, lambda z: z ^ 6)):
        total = total + lax.ppermute(got[:, i], FAR, z_pairs(move))
    total = total.transpose(1, 2, 0, 3).reshape(2, 8, G * HD).astype(BF16)
    return att, dq, total[0], total[1]


def solution(mesh):
    fine = Mesh(mesh.devices.reshape(2, 2, 4, 2, 4, 2), AXES)
    text, video = ("za", "zb", "y", "c"), ("x", "zh")
    return jax.shard_map(
        local,
        mesh=fine,
        in_specs=(P(text, None), P(video, None), P(video, None), P(text, None), P(text), P(text, None)),
        out_specs=(P(text, video), P(text, video), P(video + text, None), P(video + text, None)),
        check_vma=False,
    )
```
